32 devices in a mesh: sample: 4 (over y, x), seq: 4 (over z), head: 2 (over core).
Axes of the slice: x: 2, y: 2, z: 4, core: 2. Of those that a mesh axis runs over, the one named last changes fastest.
Arguments:
- values: bfloat16 [4, 2048, 4096], P('sample', 'seq', 'head'), may hold values from -6 to 6
- gate_values: bfloat16 [4, 2048, 4096], P('sample', 'seq', 'head'), may hold values from -6 to 6
- state_in: bfloat16 [4, 2048, 128], P('sample', 'seq'), may hold values from -0.5 to 0.5
- state_out: bfloat16 [4, 2048, 128], P('sample', 'seq'), may hold values from -0.5 to 0.5
- step_size: float32 [4, 2048, 64], P('sample', 'seq', 'head'), may hold values from 0.25 to 1
- log_decay: float32 [4, 2048, 64], P('sample', 'seq', 'head'), may hold values from -1 to 0, as said below
- skip_gain: float32 [64], P('head'), may hold values from 0.5 to 1.5
- norm_gain: float32 [4096], P('head'), may hold values from 0.25 to 1.75
- out_weight: bfloat16 [4096, 4096], P('head', 'seq'), may hold values from -0.09375 to 0.09375
- prompt_state: float32 [64, 64, 128], P('head', None, 'sample'), may hold values from -16 to 16
Outputs:
- projected: bfloat16 [4, 2048, 4096], P('sample', 'seq', 'head')
The draws below stay inside these ranges and needn't reach their ends.
Inputs may be any that keep to these rules, and one draw needn't show every extreme that they name: `log_decay`: every entry is negative.
All inputs are finite; a program needn't handle non-finite values.
Results may differ from the reference program's by a relative error of at most 0.019.
Values may be sent and summed in bfloat16 or wider, within the bound.
No kernel may reach another device: no remote copies, remote signals or barrier semaphores. Data moves between devices by JAX's collectives and lax.ppermute only.
A program may use at most 128 MiB of HBM per device.

```python
import math
import jax
import jax.numpy as jnp
from jax import lax

STATE_HEADS = 64
P_SIZE = 64
N = 128
DO = 4096
L = 256
GROUP_HEADS = 8
TOK_DEV = 512
HP = 4096
SAMPLE_COUNT = 4
SAMPLE_LENGTH = 2048
N_HEAD = 2


def draw_log_decay(key, part):
    random_rapid_key, random_brisk_key, random_gradual_key, random_block_key, random_token_key, random_spike_key, random_magnitude_key = jax.random.split(key, 7)
    fast_share = 0.5
    is_fast = jax.random.bernoulli(random_rapid_key, fast_share, (1, 1, STATE_HEADS))
    quick_rate = jax.random.uniform(random_brisk_key, (1, 1, STATE_HEADS), jnp.float32, 0.04, 0.08)
    slow_rate = jax.random.uniform(random_gradual_key, (1, 1, STATE_HEADS), jnp.float32, 0.05, 0.35) / SAMPLE_LENGTH
    baseline_decay_rate = jnp.where(is_fast, quick_rate, slow_rate)
    blocks = SAMPLE_LENGTH // TOK_DEV
    multiplier = jnp.exp(jax.random.uniform(random_block_key, (SAMPLE_COUNT, blocks, 1, STATE_HEADS), jnp.float32, -0.6931, 0.6931))
    multiplier = jnp.broadcast_to(multiplier, (SAMPLE_COUNT, blocks, TOK_DEV, STATE_HEADS)).reshape(SAMPLE_COUNT, SAMPLE_LENGTH, STATE_HEADS)
    jitter_amplitude = jax.random.uniform(random_token_key, (SAMPLE_COUNT, SAMPLE_LENGTH, STATE_HEADS), jnp.float32, 0.5, 1.5)
    spike_position = jax.random.randint(random_spike_key, (SAMPLE_COUNT, 2), 0, SAMPLE_LENGTH)
    token_offset = jnp.arange(SAMPLE_LENGTH)
    spike_row_indices = jnp.any(token_offset[None, :, None] == spike_position[:, None, :], axis=2)
    spike_magnitude = jax.random.uniform(random_magnitude_key, (SAMPLE_COUNT, SAMPLE_LENGTH, STATE_HEADS), jnp.float32, 0.22, 0.51)
    return -(baseline_decay_rate * multiplier * jitter_amplitude) - spike_row_indices[:, :, None].astype(jnp.float32) * spike_magnitude


def shard_levels(rng, shape, cuts, low, largest):
    level = 1.0
    for axis_at, parts in cuts:
        heights = jax.random.uniform(jax.random.fold_in(jax.random.fold_in(rng, 6), axis_at), (parts,), jnp.float32, low / len(cuts), largest / len(cuts))
        level = level * jnp.repeat(jnp.exp(heights), shape[axis_at] // parts).reshape((-1,) + (1,) * (len(shape) - 1 - axis_at))
    return level


def bell_draw(rng, dims, scale, reach, cuts=(), dtype=jnp.bfloat16):
    drawn = jax.random.normal(rng, dims, jnp.float32) * scale
    if len(cuts) > 0:
        drawn = shard_levels(rng, dims, cuts, -0.22, 0.18) * drawn
    return jnp.clip(drawn, min=-reach, max=reach).astype(dtype)


def setup_inputs(seed: int = 0) -> dict:
    key_list = jax.random.split(jax.random.key(seed), 11)
    return {
        "values": bell_draw(key_list[0], (SAMPLE_COUNT, SAMPLE_LENGTH, HP), 1.0, 6.0, ((0, 4), (1, 4), (2, 2))),
        "gate_values": bell_draw(key_list[1], (SAMPLE_COUNT, SAMPLE_LENGTH, HP), 1.0, 6.0, ((0, 4), (1, 4), (2, 2))),
        "state_in": bell_draw(key_list[2], (SAMPLE_COUNT, SAMPLE_LENGTH, N), N ** -0.5, 0.5, ((0, 4), (1, 4))),
        "state_out": bell_draw(key_list[3], (SAMPLE_COUNT, SAMPLE_LENGTH, N), N ** -0.5, 0.5, ((0, 4), (1, 4))),
        "step_size": jnp.clip(jnp.exp(math.log(1.0) - 1.3862944 * jax.random.uniform(key_list[4], (SAMPLE_COUNT, SAMPLE_LENGTH, STATE_HEADS), jnp.float32) ** shard_levels(key_list[4], (SAMPLE_COUNT, SAMPLE_LENGTH, STATE_HEADS), ((0, 4), (1, 4), (2, 2)), -0.2, 0.2)), 0.25, 1.0),
        "log_decay": draw_log_decay(jax.random.fold_in(key_list[10], 71), 0),
        "skip_gain": jnp.clip(0.5 + 1.0 * jax.random.uniform(key_list[6], (STATE_HEADS,), jnp.float32) ** shard_levels(key_list[6], (STATE_HEADS,), ((0, 2),), -0.2, 0.2), 0.5, 1.5),
        "norm_gain": jnp.clip(1.0 + 0.15 * jax.random.normal(key_list[7], (HP,), jnp.float32), 0.25, 1.75),
        "out_weight": bell_draw(key_list[8], (HP, DO), HP ** -0.5, 0.09375, ((0, 2), (1, 4))),
        "prompt_state": bell_draw(key_list[9], (STATE_HEADS, P_SIZE, N), 3.0, 16.0, ((0, 2), (2, 4)), jnp.float32),
    }


EPSILON = 1e-05

def block_terms(values_blk, in_blk, out_blk, step_blk, decay_blk, skip_gain):
    heads = decay_blk.shape[1]
    running = jnp.cumsum(decay_blk, axis=0)
    per_head = values_blk.reshape(values_blk.shape[0], heads, -1)
    scaled = (per_head.astype(jnp.float32) * step_blk[:, :, None]).astype(jnp.bfloat16)
    scores = jnp.dot(out_blk, in_blk.T, preferred_element_type=jnp.float32)
    token_offset = jnp.arange(values_blk.shape[0])
    causal = token_offset[:, None] >= token_offset[None, :]
    by_head = running.T
    spread = by_head[:, :, None] - by_head[:, None, :]
    pair_decay = jnp.exp(jnp.where(causal[None], spread, -1e+30))
    mixing = (scores[None] * pair_decay).astype(jnp.bfloat16)
    inner = jnp.einsum('hts,shp->thp', mixing.astype(jnp.float32), scaled.astype(jnp.float32), precision=lax.Precision.HIGHEST)
    tail = jnp.exp(running[-1][None, :] - running)
    weighted = (scaled.astype(jnp.float32) * tail[:, :, None]).astype(jnp.bfloat16)
    block_state = jnp.einsum('shp,sn->hpn', weighted.astype(jnp.float32), in_blk.astype(jnp.float32), precision=lax.Precision.HIGHEST)
    local_out = inner + skip_gain[None, :, None] * per_head.astype(jnp.float32)
    return (local_out, running, block_state)

def group_norm(gated, norm_gain):
    width = GROUP_HEADS * P_SIZE
    grouped = gated.reshape(gated.shape[0], -1, width)
    mean_square = lax.optimization_barrier(jnp.mean(grouped * grouped, axis=-1, keepdims=True))
    rescaled = grouped * lax.rsqrt(mean_square + EPSILON)
    return (rescaled.reshape(gated.shape) * norm_gain).astype(jnp.bfloat16)

def reference(values, gate_values, state_in, state_out, step_size, log_decay, skip_gain, norm_gain, out_weight, prompt_state):
    count = SAMPLE_LENGTH // L

    def one_sample(inputs):
        values_s, gate_s, in_s, out_s, step_s, decay_s = inputs
        blocks = (values_s.reshape(count, L, -1), in_s.reshape(count, L, -1), out_s.reshape(count, L, -1), step_s.reshape(count, L, -1), decay_s.reshape(count, L, -1))

        def advance(state, block):
            values_blk, in_blk, out_blk, step_blk, decay_blk = block
            local_out, running, block_state = block_terms(values_blk, in_blk, out_blk, step_blk, decay_blk, skip_gain)
            state_low = state.astype(jnp.bfloat16).astype(jnp.float32)
            carried = jnp.exp(running)[:, :, None] * jnp.einsum('tn,hpn->thp', out_blk.astype(jnp.float32), state_low, precision=lax.Precision.HIGHEST)
            new_state = jnp.exp(running[-1])[:, None, None] * state + block_state
            return (new_state, local_out + carried)
        final_state, outputs = lax.scan(advance, prompt_state, blocks)
        outputs = outputs.reshape(SAMPLE_LENGTH, HP)
        gated = outputs * jax.nn.silu(gate_s.astype(jnp.float32))
        normed = group_norm(gated, norm_gain)
        rows = HP // N_HEAD
        total = jnp.zeros((SAMPLE_LENGTH, DO), jnp.float32)
        for shard in range(N_HEAD):
            partial_sum = jnp.dot(normed[:, shard * rows:(shard + 1) * rows], out_weight[shard * rows:(shard + 1) * rows], preferred_element_type=jnp.float32)
            partial_sum = lax.optimization_barrier(partial_sum.astype(jnp.bfloat16))
            total = total + partial_sum.astype(jnp.float32)
        return total.astype(jnp.bfloat16)
    return lax.map(one_sample, (values, gate_values, state_in, state_out, step_size, log_decay))
```

```python
from functools import partial

import jax
import jax.numpy as jnp
from jax import lax
from jax.experimental import pallas as pl
from jax.experimental.pallas import tpu as pltpu
from jax.sharding import PartitionSpec as P

P_SIZE = 64
L = 256
GROUP_HEADS = 8
WIDTH = GROUP_HEADS * P_SIZE
EPSILON = 1e-05
LOG2E = 1.4426950408889634

F32 = jnp.float32
BF16 = jnp.bfloat16


def dot(a, b, **kw):
    return jnp.dot(a, b, preferred_element_type=F32, **kw)


def spread(cols):
    rows, heads = cols.shape
    low = lax.broadcasted_iota(jnp.int32, (rows, 2 * P_SIZE), 1) < P_SIZE
    pairs = [
        jnp.where(
            low,
            jnp.broadcast_to(cols[:, j : j + 1], (rows, 2 * P_SIZE)),
            jnp.broadcast_to(cols[:, j + 1 : j + 2], (rows, 2 * P_SIZE)),
        )
        for j in range(0, heads, 2)
    ]
    return jnp.concatenate(pairs, axis=1)


def lower_ones(size):
    return (
        lax.broadcasted_iota(jnp.int32, (size, size), 0)
        >= lax.broadcasted_iota(jnp.int32, (size, size), 1)
    ).astype(F32)


def states_kernel(values_ref, step_ref, decay_ref, in_ref, bs_ref, last_ref, total_ref, wt_ref, dec_ref):
    tokens = values_ref.shape[1]
    count = tokens // L
    groups = wt_ref.shape[0]
    g = pl.program_id(1)

    @pl.when(g == 0)
    def _():
        tri = lower_ones(L)
        for b in range(count):
            rows = slice(b * L, (b + 1) * L)
            running = dot(tri, decay_ref[0, rows, :], precision=lax.Precision.HIGHEST)
            tail = jnp.exp(running[L - 1 : L, :] - running)
            step = step_ref[0, rows, :]
            ends = jnp.exp(running[L - 8 : L, :])
            for q in range(groups):
                hs = slice(q * GROUP_HEADS, (q + 1) * GROUP_HEADS)
                wt_ref[q, 0, rows, :] = step[:, hs]
                wt_ref[q, 1, rows, :] = tail[:, hs]
                dec_ref[q, b, :, :] = ends[:, hs]

    state = None
    total = None
    for b in range(count):
        rows = slice(b * L, (b + 1) * L)
        scaled = (values_ref[0, rows, :].astype(F32) * spread(wt_ref[g, 0, rows, :])).astype(BF16)
        weighted = (scaled.astype(F32) * spread(wt_ref[g, 1, rows, :])).astype(BF16)
        block = lax.dot_general(
            in_ref[0, rows, :], weighted, (((0,), (0,)), ((), ())), preferred_element_type=F32
        )
        end = spread(dec_ref[g, b, :, :])[7:8, :]
        state = block if state is None else end * state + block
        total = end if total is None else total * end
        if b < count - 1:
            bs_ref[0, b, :, :] = state
    last_ref[0, :, :] = state
    total_ref[0, :, :] = jnp.broadcast_to(total, total_ref.shape[1:])


def output_kernel(
    values_ref, gate_ref, step_ref, decay_ref, in_ref, out_ref, skip_ref, gain_ref, bs_ref, entry_ref,
    normed_ref, cols_ref, rows_ref, scores_ref,
):
    tokens = values_ref.shape[1]
    count = tokens // L
    half = L // 2
    groups = rows_ref.shape[0]
    g = pl.program_id(1)

    @pl.when(g == 0)
    def _():
        tri = lower_ones(L)
        for b in range(count):
            rows = slice(b * L, (b + 1) * L)
            running = dot(tri, decay_ref[0, rows, :] * LOG2E, precision=lax.Precision.HIGHEST)
            grown = jnp.exp2(running)
            step = step_ref[0, rows, :]
            flipped = running.T
            for q in range(groups):
                hs = slice(q * GROUP_HEADS, (q + 1) * GROUP_HEADS)
                cols_ref[q, 0, rows, :] = step[:, hs]
                cols_ref[q, 1, rows, :] = running[:, hs]
                cols_ref[q, 2, rows, :] = grown[:, hs]
                rows_ref[q, b, :, :] = flipped[hs, :]
            scores = lax.dot_general(
                out_ref[0, rows, :], in_ref[0, rows, :], (((1,), (1,)), ((), ())), preferred_element_type=F32
            )
            scores_ref[b, :, :] = jnp.where(tri > 0, scores, 0.0)

    low = lax.broadcasted_iota(jnp.int32, (L, 2 * P_SIZE), 1) < P_SIZE
    state = entry_ref[0, :, :].astype(F32)
    for b in range(count):
        rows = slice(b * L, (b + 1) * L)
        values = values_ref[0, rows, :].astype(F32)
        scaled = (values * spread(cols_ref[g, 0, rows, :])).astype(BF16)
        grown = spread(cols_ref[g, 2, rows, :])
        if b > 0:
            before = bs_ref[0, b - 1, :, :]
            start = state + before
        else:
            start = state
        carried = grown * dot(out_ref[0, rows, :], start.astype(BF16))
        state = grown[L - 1 : L, :] * state
        running = cols_ref[g, 1, rows, :]
        flipped = rows_ref[g, b, :, :]
        s00 = scores_ref[b, :half, :half]
        s10 = scores_ref[b, half:, :half]
        s11 = scores_ref[b, half:, half:]
        pieces = []
        for j in range(0, GROUP_HEADS, 2):
            lanes = slice(j * P_SIZE, (j + 2) * P_SIZE)
            pair = scaled[:, lanes]
            both = []
            for i in (j, j + 1):
                col0 = jnp.broadcast_to(running[:half, i : i + 1], (half, half))
                col1 = jnp.broadcast_to(running[half:, i : i + 1], (half, half))
                row0 = flipped[i : i + 1, :half]
                row1 = flipped[i : i + 1, half:]
                m00 = (s00 * jnp.exp2(jnp.minimum(col0 - row0, 0.0))).astype(BF16)
                m10 = (s10 * jnp.exp2(jnp.minimum(col1 - row0, 0.0))).astype(BF16)
                m11 = (s11 * jnp.exp2(jnp.minimum(col1 - row1, 0.0))).astype(BF16)
                top = dot(m00, pair[:half, :])
                bottom = dot(jnp.concatenate([m10, m11], axis=1), pair)
                both.append(jnp.concatenate([top, bottom], axis=0))
            pieces.append(jnp.where(low, both[0], both[1]))
        inner = jnp.concatenate(pieces, axis=1)
        outputs = inner + skip_ref[:, :] * values + carried
        gate = gate_ref[0, rows, :].astype(F32)
        gated = outputs * (gate * (0.5 * jnp.tanh(0.5 * gate) + 0.5))
        square = jnp.sum(gated * gated, axis=1, keepdims=True) * (1.0 / WIDTH)
        normed = gated * lax.rsqrt(square + EPSILON) * gain_ref[:, :]
        normed_ref[0, rows, :] = normed.astype(BF16)


def call_states(values, step, decay, state_in):
    samples, tokens, channels = values.shape
    heads = step.shape[-1]
    n = state_in.shape[-1]
    groups = channels // WIDTH
    count = tokens // L
    wide = pl.BlockSpec((1, tokens, WIDTH), lambda s, g: (s, 0, g))
    per_head = pl.BlockSpec((1, tokens, heads), lambda s, g: (s, 0, 0))
    small = pl.BlockSpec((1, tokens, n), lambda s, g: (s, 0, 0))
    kept = max(count - 1, 1)
    return pl.pallas_call(
        states_kernel,
        grid=(samples, groups),
        in_specs=[wide, per_head, per_head, small],
        out_specs=[
            pl.BlockSpec((1, kept, n, WIDTH), lambda s, g: (s, 0, 0, g)),
            pl.BlockSpec((1, n, WIDTH), lambda s, g: (s, 0, g)),
            pl.BlockSpec((1, 8, WIDTH), lambda s, g: (s, 0, g)),
        ],
        out_shape=[
            jax.ShapeDtypeStruct((samples, kept, n, channels), F32),
            jax.ShapeDtypeStruct((samples, n, channels), F32),
            jax.ShapeDtypeStruct((samples, 8, channels), F32),
        ],
        scratch_shapes=[
            pltpu.VMEM((groups, 2, tokens, GROUP_HEADS), F32),
            pltpu.VMEM((groups, count, 8, GROUP_HEADS), F32),
        ],
        name="block_states",
    )(values, step, decay, state_in)


def call_outputs(values, gates, step, decay, state_in, state_out, skip, gain, states, entry):
    samples, tokens, channels = values.shape
    heads = step.shape[-1]
    n = state_in.shape[-1]
    groups = channels // WIDTH
    count = tokens // L
    wide = pl.BlockSpec((1, tokens, WIDTH), lambda s, g: (s, 0, g))
    per_head = pl.BlockSpec((1, tokens, heads), lambda s, g: (s, 0, 0))
    small = pl.BlockSpec((1, tokens, n), lambda s, g: (s, 0, 0))
    row = pl.BlockSpec((1, WIDTH), lambda s, g: (0, g))
    return pl.pallas_call(
        output_kernel,
        grid=(samples, groups),
        in_specs=[
            wide, wide, per_head, per_head, small, small, row, row,
            pl.BlockSpec((1, states.shape[1], n, WIDTH), lambda s, g: (s, 0, 0, g)),
            pl.BlockSpec((1, n, WIDTH), lambda s, g: (s, 0, g)),
        ],
        out_specs=wide,
        out_shape=jax.ShapeDtypeStruct((samples, tokens, channels), BF16),
        scratch_shapes=[
            pltpu.VMEM((groups, 3, tokens, GROUP_HEADS), F32),
            pltpu.VMEM((groups, count, GROUP_HEADS, L), F32),
            pltpu.VMEM((count, L, L), F32),
        ],
        name="local_outputs",
    )(values, gates, step, decay, state_in, state_out, skip, gain, states, entry)


def project_kernel(layout, place_ref, normed_ref, *refs):
    out_ref = refs[-1]
    pieces = refs[:-1]
    at = 0
    for offset, parts in layout:
        total = None
        row = 0
        for _ in range(parts):
            piece = pieces[at]
            at += 1
            term = dot(normed_ref[:, row : row + piece.shape[0]], piece[:, :])
            row += piece.shape[0]
            total = term if total is None else total + term
        width = total.shape[1]
        if isinstance(offset, int):
            start = offset
        else:
            start = pl.multiple_of(place_ref[offset[0]] * width, 128)
        out_ref[:, pl.ds(start, width)] = total.astype(BF16)


def call_project(normed, pieces, layout, columns, places):
    rows, depth = normed.shape
    tile = min(rows, 512)
    return pl.pallas_call(
        partial(project_kernel, layout),
        grid_spec=pltpu.PrefetchScalarGridSpec(
            num_scalar_prefetch=1,
            grid=(rows // tile,),
            in_specs=[pl.BlockSpec((tile, depth), lambda i, p: (i, 0))]
            + [pl.BlockSpec(piece.shape, lambda i, p: (0, 0)) for piece in pieces],
            out_specs=pl.BlockSpec((tile, columns), lambda i, p: (i, 0)),
        ),
        out_shape=jax.ShapeDtypeStruct((rows, columns), BF16),
        name="project",
    )(places, normed, *pieces)


def finish_kernel(place_ref, *refs):
    out_ref = refs[-1]
    pairs = len(refs) // 2
    for k in range(pairs):
        width = refs[k].shape[1]
        start = pl.multiple_of(place_ref[k] * width, 128)
        out_ref[:, pl.ds(start, width)] = (
            refs[k][:, :].astype(F32) + refs[pairs + k][:, :].astype(F32)
        ).astype(BF16)


def call_finish(kept, received, places):
    rows, width = kept[0].shape
    tile = min(rows, 512)
    spec = pl.BlockSpec((tile, width), lambda i, p: (i, 0))
    return pl.pallas_call(
        finish_kernel,
        grid_spec=pltpu.PrefetchScalarGridSpec(
            num_scalar_prefetch=1,
            grid=(rows // tile,),
            in_specs=[spec] * (2 * len(kept)),
            out_specs=pl.BlockSpec((tile, width * len(kept)), lambda i, p: (i, 0)),
        ),
        out_shape=jax.ShapeDtypeStruct((rows, width * len(kept)), BF16),
        name="finish",
    )(places, *kept, *received)


def flip(array, axis, size, bit):
    return lax.ppermute(array, axis, [(i, i ^ bit) for i in range(size)])


def in_plane(piece, size):
    mid = piece.shape[0] // 2
    by_x = flip(piece, "sample", size, 1)
    by_y = flip(piece, "sample", size, 2)
    far_a = flip(by_y[:mid], "sample", size, 1)
    far_b = flip(by_x[mid:], "sample", size, 2)
    return [piece, by_x, by_y, far_a, far_b]


def shards(
    sizes,
    values,
    gate_values,
    state_in,
    state_out,
    step_size,
    log_decay,
    skip_gain,
    norm_gain,
    out_weight,
    prompt_state,
):
    n_sample, n_seq, n_head = sizes
    me_s = lax.axis_index("sample")
    me_z = lax.axis_index("seq")
    me_h = lax.axis_index("head")
    samples, tokens, channels = values.shape
    heads = step_size.shape[-1]

    depth, columns = out_weight.shape
    wide = columns // n_sample
    thin = wide // 2
    direct = columns // 2
    own_thin = lax.dynamic_slice_in_dim(out_weight, me_s * thin, thin, 1)
    own_wide = lax.dynamic_slice_in_dim(out_weight, me_s * wide, wide, 1)
    got = {0: own_wide, 1: flip(own_thin, "seq", n_seq, 1)}
    for k in range(2, n_seq):
        bit = k & -k
        got[k] = flip(got[k ^ bit], "seq", n_seq, bit)
    slots = {k: in_plane(got[k], n_sample) for k in range(1, n_seq)}
    rest = lax.optimization_barrier((out_weight[:, direct:], got[n_seq - 1]))[0]
    rest = flip(rest, "seq", n_seq, 1)

    states, last, total = call_states(values, step_size, log_decay, state_in)
    total = total[:, :1, :]
    mine = prompt_state.astype(BF16).reshape(channels, -1).T
    by_x = flip(mine, "sample", n_sample, 1)
    by_y = flip(jnp.stack([mine, by_x]), "sample", n_sample, 2)
    parts = jnp.stack([mine, by_x, by_y[0], by_y[1]])
    prompt = jnp.concatenate(
        [lax.dynamic_index_in_dim(parts, me_s ^ i, 0, False) for i in range(n_sample)], axis=0
    )
    first = jnp.where(me_z == 0, prompt, jnp.zeros_like(prompt))
    entry = jnp.broadcast_to(first[None], last.shape)
    for k in range(n_seq - 1):
        sent = (total * entry.astype(F32) + last).astype(BF16)
        entry = entry + lax.ppermute(sent, "seq", [(k, k + 1)])

    skip = jnp.repeat(skip_gain, P_SIZE)[None]
    normed = call_outputs(
        values, gate_values, step_size, log_decay, state_in, state_out, skip, norm_gain[None], states, entry
    ).reshape(samples * tokens, channels)

    places = jnp.stack([me_s, me_s ^ 1, me_s ^ 2, me_s ^ 3]).astype(jnp.int32)
    spots = tuple(((i,), 1) for i in range(3)) + (((3,), 2),)
    made = {0: call_project(normed, [out_weight], ((0, 1),), columns, places)}
    for k in range(1, n_seq):
        if k == 1:
            made[k] = call_project(normed, slots[k] + [rest], spots + ((direct, 1),), columns, places)
        else:
            made[k] = call_project(normed, slots[k], spots, columns, places)
    pairs = n_seq // 2
    same = me_h == me_z // pairs
    kept, received = [], []
    for k in range(pairs):
        kept.append(jnp.where(same, made[k], made[k + pairs]))
        sent = jnp.where(same, made[k + pairs], made[k])
        received.append(flip(sent, "head", n_head, 1))
    spots = jnp.stack([(me_z ^ k) % pairs for k in range(pairs)]).astype(jnp.int32)
    return call_finish(kept, received, spots).reshape(samples, tokens, -1)


def solution(mesh):
    in_specs = (
        P("sample", "seq", "head"),
        P("sample", "seq", "head"),
        P("sample", "seq", None),
        P("sample", "seq", None),
        P("sample", "seq", "head"),
        P("sample", "seq", "head"),
        P("head"),
        P("head"),
        P("head", "seq"),
        P("head", None, "sample"),
    )
    out_specs = P("sample", "seq", "head")
    sizes = tuple(mesh.shape[a] for a in ("sample", "seq", "head"))
    return jax.shard_map(
        partial(shards, sizes), mesh=mesh, in_specs=in_specs, out_specs=out_specs, check_vma=False
    )
```
